32 devices in a mesh: expert: 4 (over x, core), ctx: 2 (over y), tensor: 4 (over z).
Axes of the slice: x: 2, y: 2, z: 4, core: 2. Of those that a mesh axis runs over, the one named last changes fastest.
Arguments:
- tokens: bfloat16 [64, 6144], P('expert', 'tensor'), may hold values from -6 to 6
- expert_ids: int32 [64, 2], P('expert'), may hold values from 0 to 3, all different within a row; in each aligned block of 8 rows (0 to 7, 8 to 15, ...) at most 4 rows name the same one
- route_gates: float32 [64, 2], P('expert'), may hold values from 0.2 to 1
- up_weight: bfloat16 [4, 12288, 6144], P('expert', 'ctx', 'tensor'), may hold values from -0.078125 to 0.078125
- down_weight: bfloat16 [4, 12288, 6144], P('expert', 'ctx', 'tensor'), may hold values from -0.0546875 to 0.0546875
Outputs:
- mixed: bfloat16 [64, 6144], P(('expert', 'ctx'), 'tensor')
The draws below stay inside these ranges and needn't reach their ends.
Inputs may be any that keep to these rules, and one draw needn't show every extreme that they name: `expert_ids`: each token names 2 different experts. In each aligned block of 8 tokens at most 4 choices name one expert, and in some block one expert is named exactly 4 times. Every expert is named somewhere.
All inputs are finite; a program needn't handle non-finite values.
Results may differ from the reference program's by a relative error of at most 0.0057.
Values may be sent and summed in bfloat16 or wider, within the bound.
No kernel may reach another device: no remote copies, remote signals or barrier semaphores. Data moves between devices by JAX's collectives and lax.ppermute only.
A program may use at most 64 MiB of HBM per device.

```python
import math
import jax
import jax.numpy as jnp
import numpy as np
from jax import lax

D = 6144
FF = 12288
TOPK = 2
TB = 8
CAP = 4
EXPERTS = 4
TOKENS = 64


def block_scale(key, extent, split, low, top_value):
    def one(dim, parts):
        heights = jax.random.uniform(jax.random.fold_in(jax.random.fold_in(key, 6), dim), (parts,), jnp.float32, low / len(split), top_value / len(split))
        return jnp.repeat(jnp.exp(heights), extent[dim] // parts).reshape((-1,) + (1,) * (len(extent) - dim - 1))

    loudness = one(*split[0])
    for cut in split[1:]:
        loudness = loudness * one(*cut)
    return loudness


def assign_block(key, own, number, rows, count, top, bound, lean):
    order = jax.random.permutation(key, count)
    heavy_load, ordinary = load_shares(count, rows * top, bound, lean, True), load_shares(count, rows * top, bound, lean, False)
    places = jnp.arange(count)

    def named(tallies, turn):
        used = int((tallies > 0).sum())
        fixed = max(1, used // 4)
        moved = fixed + (places - fixed + turn * (used - fixed)) % max(1, count - fixed)
        return jnp.zeros((count,), jnp.int32).at[order[jnp.where(places < fixed, places, moved)]].set(jnp.asarray(tallies, jnp.int32))

    tallies = jnp.where(number % 4 == 0, named(heavy_load, number // 4), named(ordinary, number - number // 4 - 1))
    mixed = jax.random.permutation(jax.random.fold_in(own, 3), count)
    giver, receiver = mixed[0:count // 2 * 2:2], mixed[1:count // 2 * 2:2]
    slack = jnp.minimum(tallies[giver] - 1, bound - tallies[receiver]) // 2
    slack = jnp.where((giver == order[0]) | (receiver == order[0]) | (tallies[receiver] == 0), 0, jnp.maximum(slack, 0))
    moved = jax.random.randint(jax.random.fold_in(own, 4), (count // 2,), 0, 1 << 20) % (slack + 1)
    tallies = tallies.at[giver].add(-moved).at[receiver].add(moved)
    items = jnp.searchsorted(jnp.cumsum(tallies), jnp.arange(rows * top), side="right").astype(jnp.int32)
    table = items.reshape(top, rows).T
    table = table[jax.random.permutation(jax.random.fold_in(own, 1), rows)]
    turn = jax.random.randint(jax.random.fold_in(own, 2), (rows, 1), 0, top)
    return jnp.take_along_axis(table, (jnp.arange(top)[None, :] + turn) % top, axis=1)


def load_shares(amount, total, most, lean, full):
    loads = [(1 << 20) // math.isqrt(rank ** lean) + 1 for rank in range(1, amount + 1)]
    largest = most if full else min(most, max(-(-total // amount), total * loads[0] // sum(loads)))
    least = 1 if total - largest >= amount - 1 else 0
    given, surplus = [largest] + [least] * (amount - 1), total - largest - least * (amount - 1)
    while surplus > 0:
        candidates = [i for i in range(1, amount) if given[i] < largest] or [i for i in range(1, amount) if given[i] < most]
        pool, left = sum([loads[i] for i in candidates]), surplus
        for i in candidates:
            more = min(most - given[i], max(1, left * loads[i] // pool), surplus)
            given[i] = given[i] + more
            surplus = surplus - more
    return np.array(given)


def gaussian(own_key, extent, width, limit, shards=(), held_as=jnp.bfloat16):
    result = jax.random.normal(own_key, extent, jnp.float32) * width
    if len(shards) > 0:
        result = block_scale(own_key, extent, shards, -0.22, 0.18) * result
    return jnp.clip(result, min=-limit, max=limit).astype(held_as)


def setup_inputs(seed: int = 0) -> dict:
    arg_keys = jax.random.split(jax.random.key(seed), 6)
    tokens = gaussian(arg_keys[0], (TOKENS, D), 1.0, 6.0, ((0, 4), (1, 4)))
    expert_ids_keys = jax.random.split(jax.random.fold_in(arg_keys[1], 1), TOKENS // TB)
    expert_ids_turns = jax.random.permutation(jax.random.fold_in(arg_keys[1], 3), TOKENS // TB)
    expert_ids = jax.vmap(lambda own, number: assign_block(jax.random.fold_in(arg_keys[1], 2), own, number, TB, EXPERTS, TOPK, CAP, 2))(expert_ids_keys, expert_ids_turns).reshape((TOKENS, TOPK))
    route_gates = jnp.clip(0.2 + 0.8 * jax.random.uniform(arg_keys[2], (TOKENS, TOPK), jnp.float32) ** block_scale(arg_keys[2], (TOKENS, TOPK), ((0, 4),), -0.2, 0.2), 0.2, 1.0)
    up_weight = gaussian(arg_keys[3], (EXPERTS, FF, D), D ** -0.5, 0.078125, ((0, 4), (1, 2), (2, 4)))
    down_weight = gaussian(arg_keys[4], (EXPERTS, FF, D), FF ** -0.5, 0.0546875, ((0, 4), (1, 2), (2, 4)))
    return dict(tokens=tokens, expert_ids=expert_ids, route_gates=route_gates, up_weight=up_weight, down_weight=down_weight)


def choice_slots(expert_ids):
    per_block = expert_ids.reshape(-1, TB * TOPK)
    marked = (per_block[:, :, None] == jnp.arange(EXPERTS, dtype=jnp.int32)[None, None, :]).astype(jnp.int32)
    earlier = jnp.cumsum(marked, axis=1) - marked
    return jnp.sum(earlier * marked, axis=2).astype(jnp.int32).reshape(-1, TOPK)


def expert_ffn(operands):
    expert_rows, up_slice, down_slice = operands
    before_act = jnp.dot(expert_rows, up_slice.T, preferred_element_type=jnp.float32)
    hidden = jnp.square(jnp.maximum(before_act, 0.0)).astype(jnp.bfloat16)
    return jnp.dot(hidden, down_slice, preferred_element_type=jnp.float32).astype(jnp.bfloat16)


def reference(tokens, expert_ids, route_gates, up_weight, down_weight):
    slot_ids = choice_slots(expert_ids)
    block_of = (jnp.arange(TOKENS, dtype=jnp.int32) // TB)[:, None]
    target = (block_of * CAP + slot_ids).astype(jnp.int32)
    buffers = jnp.zeros((EXPERTS, (TOKENS // TB) * CAP, D), jnp.bfloat16)
    copies = jnp.broadcast_to(tokens[:, None, :], (TOKENS, TOPK, D))
    buffers = buffers.at[expert_ids, target].set(copies)
    results = lax.map(expert_ffn, (buffers, up_weight, down_weight))
    picked = results[expert_ids, target].astype(jnp.float32)
    mixed = jnp.sum(route_gates.astype(jnp.float32)[:, :, None] * picked, axis=1)
    return mixed.astype(jnp.bfloat16)
```

```python
import functools

import jax
import jax.numpy as jnp
from jax import lax
from jax.experimental import pallas as pl
from jax.experimental.pallas import tpu as pltpu
from jax.sharding import PartitionSpec as P

VMEM = pl.BlockSpec(memory_space=pltpu.VMEM)
MIB = 1 << 20
AHEAD = 1 << 34


def shift_of(size):
    return size.bit_length() - 1


def vmem_call(body, args, outs, name, flops=0, moved=0, limit=4 * MIB):
    return pl.pallas_call(
        body,
        in_specs=[VMEM] * len(args),
        out_specs=jax.tree.map(lambda _: VMEM, outs),
        out_shape=outs,
        name=name,
        cost_estimate=pl.CostEstimate(flops=flops, transcendentals=0, bytes_accessed=moved),
        compiler_params=pltpu.CompilerParams(vmem_limit_bytes=limit),
    )(*args)


def named_before(ids, expert_row, block_len):
    count = ids.shape[0]
    first = ids[:, 0:1] == expert_row
    second = ids[:, 1:2] == expert_row
    names = jnp.where(first | second, 1.0, 0.0)
    row = lax.broadcasted_iota(jnp.int32, (count, count), 0)
    col = lax.broadcasted_iota(jnp.int32, (count, count), 1)
    shift = shift_of(block_len)
    earlier = (col < row) & (lax.shift_right_logical(row, shift) == lax.shift_right_logical(col, shift))
    slot = jnp.dot(
        jnp.where(earlier, 1.0, 0.0).astype(jnp.bfloat16),
        names.astype(jnp.bfloat16),
        preferred_element_type=jnp.float32,
    )
    return first, second, names, slot


def dispatch_body(tokens_ref, ids_ref, *out_refs, block_len, capacity, per_expert):
    ids = ids_ref[...]
    group_len = ids.shape[0]
    lanes = per_expert * len(out_refs)
    lane = lax.broadcasted_iota(jnp.int32, (1, lanes), 1)
    expert_row = lax.axis_index("expert") ^ lax.shift_right_logical(lane, shift_of(per_expert))
    _, _, names, slot = named_before(ids, expert_row, block_len)
    want_slot = (lane & (capacity - 1)).astype(jnp.float32)
    want_block = lax.shift_right_logical(lane, shift_of(capacity)) & (per_expert // capacity - 1)
    token = lax.broadcasted_iota(jnp.int32, (group_len, lanes), 0)
    hit = (names > 0) & (slot == want_slot) & (lax.shift_right_logical(token, shift_of(block_len)) == want_block)
    rows = lax.dot_general(
        jnp.where(hit, 1.0, 0.0).astype(jnp.bfloat16),
        tokens_ref[...],
        (((0,), (0,)), ((), ())),
        preferred_element_type=jnp.float32,
    ).astype(jnp.bfloat16)
    for k, ref in enumerate(out_refs):
        ref[...] = rows[k * per_expert:(k + 1) * per_expert]


def up_body(*refs, step, chunk):
    *row_refs, up_ref, out_ref = refs
    rows = jnp.concatenate([ref[...] for ref in row_refs], axis=0)
    start = pl.multiple_of((lax.axis_index("tensor") ^ step) * chunk, chunk)
    out_ref[...] = lax.dot_general(
        rows, up_ref[pl.ds(start, chunk), :], (((1,), (1,)), ((), ())), preferred_element_type=jnp.float32
    ).astype(out_ref.dtype)


def act_body(*refs):
    *part_refs, out_ref = refs
    total = part_refs[0][...].astype(jnp.float32)
    for ref in part_refs[1:]:
        total = total + ref[...].astype(jnp.float32)
    out_ref[...] = jnp.square(jnp.maximum(total, 0.0)).astype(jnp.bfloat16)


def down_body(*refs, step, chunk):
    hidden_ref, down_ref, *prior, out_ref = refs
    start = pl.multiple_of((lax.axis_index("tensor") ^ step) * chunk, chunk)
    total = jnp.dot(hidden_ref[...], down_ref[pl.ds(start, chunk), :], preferred_element_type=jnp.float32)
    if prior:
        total = total + prior[0][...]
    out_ref[...] = total


def last_body(hidden_ref, down_ref, prior_ref, out_ref, *, step, chunk, ctx_count, capacity):
    start = pl.multiple_of((lax.axis_index("tensor") ^ step) * chunk, chunk)
    total = prior_ref[...] + jnp.dot(
        hidden_ref[...], down_ref[pl.ds(start, chunk), :], preferred_element_type=jnp.float32
    )
    mine = lax.axis_index("expert")
    for piece in range(total.shape[0] // capacity):
        k, b = piece // ctx_count, piece % ctx_count
        dest = (mine ^ k) * ctx_count + b
        out_ref[dest] = total[piece * capacity:(piece + 1) * capacity].astype(out_ref.dtype)


def mix_body(back_ref, ids_ref, gates_ref, out_ref, *, block_len, capacity, ctx_count):
    lanes_all = back_ref.shape[0]
    expert_count = lanes_all // ctx_count
    picked = []
    for e in range(expert_count):
        total = back_ref[e * ctx_count].astype(jnp.float32)
        for c in range(1, ctx_count):
            total = total + back_ref[e * ctx_count + c].astype(jnp.float32)
        picked.append(total)
    rows = jnp.concatenate(picked, axis=0).astype(jnp.bfloat16)
    start = pl.multiple_of(lax.axis_index("ctx") * block_len, block_len)
    ids = ids_ref[pl.ds(start, block_len), :]
    gates = gates_ref[pl.ds(start, block_len), :]
    lane = lax.broadcasted_iota(jnp.int32, (1, expert_count * capacity), 1)
    first, second, _, slot = named_before(ids, lax.shift_right_logical(lane, shift_of(capacity)), block_len)
    here = slot == (lane & (capacity - 1)).astype(jnp.float32)
    mixed = 0.0
    for which, gate in ((first, gates[:, 0:1]), (second, gates[:, 1:2])):
        pick = jnp.where(which & here, 1.0, 0.0).astype(jnp.bfloat16)
        mixed = mixed + gate * jnp.dot(pick, rows, preferred_element_type=jnp.float32)
    out_ref[...] = mixed.astype(jnp.bfloat16)


def swap(x, axis, count, k):
    return lax.ppermute(x, axis, [(i, i ^ k) for i in range(count)])


def local(tokens, expert_ids, route_gates, up_weight, down_weight, *, expert_count, ctx_count, tensor_count):
    group_len, width = tokens.shape
    block_len = group_len // ctx_count
    capacity = block_len // 2
    per_expert = ctx_count * capacity
    rows = expert_count * per_expert
    hidden_local = up_weight.shape[1]
    chunk = hidden_local // tensor_count
    up_local = up_weight.reshape(up_weight.shape[1:])
    down_local = down_weight.reshape(down_weight.shape[1:])
    shape = jax.ShapeDtypeStruct
    bf16, f32 = jnp.bfloat16, jnp.float32

    outgoing = vmem_call(
        functools.partial(dispatch_body, block_len=block_len, capacity=capacity, per_expert=per_expert),
        (tokens, expert_ids),
        [shape((per_expert, width), bf16)] * expert_count,
        "dispatch",
        flops=AHEAD,
    )
    arrived = [outgoing[0]] + [swap(outgoing[k], "expert", expert_count, k) for k in range(1, expert_count)]

    flops = 2 * rows * width * chunk
    order = list(range(tensor_count - 1, 0, -1))
    parts = []
    for k in order:
        part = vmem_call(
            functools.partial(up_body, step=k, chunk=chunk), (*arrived, up_local), shape((rows, chunk), bf16),
            f"up{k}", flops,
        )
        parts.append(swap(part, "tensor", tensor_count, k))
    own = vmem_call(
        functools.partial(up_body, step=0, chunk=chunk), (*arrived, up_local), shape((rows, chunk), f32), "up0", flops
    )
    hidden = vmem_call(act_body, (own, *parts), shape((rows, chunk), bf16), "act")
    others = [(k, swap(hidden, "tensor", tensor_count, k)) for k in range(1, tensor_count)]
    total = vmem_call(
        functools.partial(down_body, step=0, chunk=chunk), (hidden, down_local), shape((rows, width), f32), "down0",
        flops,
    )
    for k, other in others[:-1]:
        total = vmem_call(
            functools.partial(down_body, step=k, chunk=chunk), (other, down_local, total), shape((rows, width), f32),
            f"down{k}", flops,
        )
    k, other = others[-1]
    leaving = vmem_call(
        functools.partial(last_body, step=k, chunk=chunk, ctx_count=ctx_count, capacity=capacity),
        (other, down_local, total),
        shape((expert_count * ctx_count, capacity, width), bf16),
        f"down{k}",
        flops,
    )
    back = lax.all_to_all(leaving, ("expert", "ctx"), 0, 0, tiled=True)
    return vmem_call(
        functools.partial(mix_body, block_len=block_len, capacity=capacity, ctx_count=ctx_count),
        (back, expert_ids, route_gates),
        shape((block_len, width), bf16),
        "mix",
    )


def solution(mesh):
    body = functools.partial(
        local,
        expert_count=mesh.shape["expert"],
        ctx_count=mesh.shape["ctx"],
        tensor_count=mesh.shape["tensor"],
    )
    in_specs = (
        P("expert", "tensor"),
        P("expert", None),
        P("expert", None),
        P("expert", "ctx", "tensor"),
        P("expert", "ctx", "tensor"),
    )
    out_specs = P(("expert", "ctx"), "tensor")
    return jax.shard_map(body, mesh=mesh, in_specs=in_specs, out_specs=out_specs, check_vma=False)
```

```python
import functools

import jax
import jax.numpy as jnp
from jax import lax
from jax.experimental import pallas as pl
from jax.experimental.pallas import tpu as pltpu
from jax.sharding import PartitionSpec as P

VMEM = pl.BlockSpec(memory_space=pltpu.VMEM)
MIB = 1 << 20
AHEAD = 1 << 34


def shift_of(size):
    return size.bit_length() - 1


def vmem_call(body, args, outs, name, flops=0, moved=0, limit=4 * MIB):
    return pl.pallas_call(
        body,
        in_specs=[VMEM] * len(args),
        out_specs=jax.tree.map(lambda _: VMEM, outs),
        out_shape=outs,
        name=name,
        cost_estimate=pl.CostEstimate(flops=flops, transcendentals=0, bytes_accessed=moved),
        compiler_params=pltpu.CompilerParams(vmem_limit_bytes=limit),
    )(*args)


def lane_iota(shape):
    return lax.broadcasted_iota(jnp.int32, shape, 1)


def row_iota(shape):
    return lax.broadcasted_iota(jnp.int32, shape, 0)


def ones_where(mask, dtype):
    return jnp.where(mask, 1.0, 0.0).astype(dtype)


def dispatch_body(tokens_hbm, ids_hbm, gates_hbm, *refs, block_len, capacity, per_expert, expert_count):
    *out_refs, pick_ref, gate_ref, tokens_ref, ids_ref, gates_ref, sem = refs
    copies = [
        pltpu.make_async_copy(src, dst, sem.at[i])
        for i, (src, dst) in enumerate(((ids_hbm, ids_ref), (gates_hbm, gates_ref), (tokens_hbm, tokens_ref)))
    ]
    for copy in copies:
        copy.start()
    copies[0].wait()
    first, second = ids_ref[0:1, :], ids_ref[1:2, :]
    group_len = first.shape[1]
    block_shift, cap_shift = shift_of(block_len), shift_of(capacity)
    count = per_expert * expert_count
    row = row_iota((count, 1))
    expert = lax.axis_index("expert") ^ lax.shift_right_logical(row, shift_of(per_expert))
    names = (first == expert) | (second == expert)
    earlier_token, token = row_iota((group_len, group_len)), lane_iota((group_len, group_len))
    before = (earlier_token < token) & (
        lax.shift_right_logical(earlier_token, block_shift) == lax.shift_right_logical(token, block_shift)
    )
    slot = jnp.dot(
        ones_where(names, jnp.bfloat16), ones_where(before, jnp.bfloat16), preferred_element_type=jnp.float32
    )
    block_of_row = lax.shift_right_logical(row, cap_shift) & (per_expert // capacity - 1)
    block_of_token = lax.shift_right_logical(lane_iota((1, group_len)), block_shift)
    hit = names & (slot == (row & (capacity - 1)).astype(jnp.float32)) & (block_of_row == block_of_token)
    copies[2].wait()
    rows = jnp.dot(
        ones_where(hit, jnp.bfloat16), tokens_ref[...], preferred_element_type=jnp.float32
    ).astype(jnp.bfloat16)
    for k, ref in enumerate(out_refs):
        ref[...] = rows[k * per_expert:(k + 1) * per_expert]

    copies[1].wait()
    own_start = lax.axis_index("ctx") * block_len
    own = row_iota((block_len, group_len)) + own_start
    lane = lane_iota((block_len, group_len))
    here = ones_where(own == lane, jnp.float32)
    ahead = (lane < own) & (lane >= own_start)
    halves = pick_ref.shape[0] // (2 * block_len)
    wide = lane_iota((block_len, pick_ref.shape[1]))
    for choice, named in enumerate((first, second)):
        chosen = jnp.sum(here * named.astype(jnp.float32), axis=1, keepdims=True).astype(jnp.int32)
        again = ahead & ((first == chosen) | (second == chosen))
        own_slot = jnp.sum(ones_where(again, jnp.float32), axis=1, keepdims=True).astype(jnp.int32)
        for half in range(halves):
            at = (half * 2 + choice) * block_len
            source = chosen * (halves * capacity) + half * capacity + own_slot
            pick_ref[at:at + block_len, :] = ones_where(wide == source, jnp.bfloat16)
        gate = jnp.sum(here * gates_ref[choice:choice + 1, :], axis=1, keepdims=True)
        gate_ref[choice * block_len:(choice + 1) * block_len, :] = jnp.broadcast_to(
            gate, (block_len, gate_ref.shape[1])
        )


def up_body(*refs, step, chunk):
    *row_refs, up_ref, out_ref = refs
    rows = jnp.concatenate([ref[...] for ref in row_refs], axis=0)
    start = pl.multiple_of((lax.axis_index("tensor") ^ step) * chunk, chunk)
    out_ref[...] = lax.dot_general(
        rows, up_ref[pl.ds(start, chunk), :], (((1,), (1,)), ((), ())), preferred_element_type=jnp.float32
    ).astype(out_ref.dtype)


def act_body(*refs):
    *part_refs, out_ref = refs
    total = part_refs[0][...].astype(jnp.float32)
    for ref in part_refs[1:]:
        total = total + ref[...].astype(jnp.float32)
    out_ref[...] = jnp.square(jnp.maximum(total, 0.0)).astype(jnp.bfloat16)


def down_body(*refs, step, chunk):
    hidden_ref, down_ref, *prior, out_ref = refs
    start = pl.multiple_of((lax.axis_index("tensor") ^ step) * chunk, chunk)
    total = jnp.dot(hidden_ref[...], down_ref[pl.ds(start, chunk), :], preferred_element_type=jnp.float32)
    if prior:
        total = total + prior[0][...]
    out_ref[...] = total


def last_body(hidden_ref, down_ref, prior_ref, out_ref, *, step, chunk, ctx_count, capacity):
    start = pl.multiple_of((lax.axis_index("tensor") ^ step) * chunk, chunk)
    total = prior_ref[...] + jnp.dot(
        hidden_ref[...], down_ref[pl.ds(start, chunk), :], preferred_element_type=jnp.float32
    )
    mine = lax.axis_index("expert")
    width = out_ref.shape[1]
    halves = total.shape[1] // width
    for piece in range(total.shape[0] // capacity):
        k, b = piece // ctx_count, piece % ctx_count
        dest = pl.multiple_of(((mine ^ k) * ctx_count + b) * (halves * capacity), halves * capacity)
        rows = total[piece * capacity:(piece + 1) * capacity]
        cut = jnp.concatenate([rows[:, h * width:(h + 1) * width] for h in range(halves)], axis=0)
        out_ref[pl.ds(dest, halves * capacity), :] = cut.astype(out_ref.dtype)


def mix_body(back_ref, pick_ref, gate_ref, out_ref, *, ctx_count, piece_len):
    width = back_ref.shape[1]
    picked = []
    for e in range(back_ref.shape[0] // (piece_len * ctx_count)):
        at = e * ctx_count * piece_len
        total = back_ref[at:at + piece_len].astype(jnp.float32)
        for c in range(1, ctx_count):
            total = total + back_ref[at + c * piece_len:at + (c + 1) * piece_len].astype(jnp.float32)
        picked.append(total)
    rows = jnp.concatenate(picked, axis=0).astype(jnp.bfloat16)
    chosen = jnp.dot(pick_ref[...], rows, preferred_element_type=jnp.float32)
    block_len = out_ref.shape[0]
    gates = gate_ref[...]
    for half in range(out_ref.shape[1] // width):
        at = half * 2 * block_len
        mixed = (
            gates[:block_len, 0:1] * chosen[at:at + block_len]
            + gates[block_len:, 0:1] * chosen[at + block_len:at + 2 * block_len]
        )
        out_ref[:, half * width:(half + 1) * width] = mixed.astype(jnp.bfloat16)


def swap(x, axis, count, k):
    return lax.ppermute(x, axis, [(i, i ^ k) for i in range(count)])


def local(tokens, expert_ids, route_gates, up_weight, down_weight, *, expert_count, ctx_count, tensor_count):
    group_len, width = tokens.shape
    block_len = group_len // ctx_count
    capacity = block_len // 2
    per_expert = ctx_count * capacity
    rows = expert_count * per_expert
    hidden_local = up_weight.shape[1]
    chunk = hidden_local // tensor_count
    up_local = up_weight.reshape(up_weight.shape[1:])
    down_local = down_weight.reshape(down_weight.shape[1:])
    shape = jax.ShapeDtypeStruct
    bf16, f32 = jnp.bfloat16, jnp.float32

    halves = max(1, 8 // capacity)
    piece_len = halves * capacity
    *outgoing, pick, gate = pl.pallas_call(
        functools.partial(
            dispatch_body, block_len=block_len, capacity=capacity, per_expert=per_expert, expert_count=expert_count
        ),
        in_specs=[pl.BlockSpec(memory_space=pltpu.HBM)] * 3,
        out_specs=[VMEM] * (expert_count + 2),
        out_shape=[shape((per_expert, width), bf16)] * expert_count
        + [shape((halves * 2 * block_len, expert_count * piece_len), bf16), shape((2 * block_len, 128), f32)],
        scratch_shapes=[
            pltpu.VMEM((group_len, width), bf16),
            pltpu.VMEM((2, group_len), jnp.int32),
            pltpu.VMEM((2, group_len), f32),
            pltpu.SemaphoreType.DMA((3,)),
        ],
        name="dispatch",
        cost_estimate=pl.CostEstimate(flops=AHEAD, transcendentals=0, bytes_accessed=0),
        compiler_params=pltpu.CompilerParams(vmem_limit_bytes=4 * MIB),
    )(*[pltpu.with_memory_space_constraint(x, pltpu.HBM) for x in (tokens, expert_ids.T, route_gates.T)])
    arrived = [outgoing[0]] + [swap(outgoing[k], "expert", expert_count, k) for k in range(1, expert_count)]

    flops = 2 * rows * width * chunk
    order = list(range(tensor_count - 1, 0, -1))
    parts = []
    for k in order:
        part = vmem_call(
            functools.partial(up_body, step=k, chunk=chunk), (*arrived, up_local), shape((rows, chunk), bf16),
            f"up{k}", flops,
        )
        parts.append(swap(part, "tensor", tensor_count, k))
    own = vmem_call(
        functools.partial(up_body, step=0, chunk=chunk), (*arrived, up_local), shape((rows, chunk), f32), "up0", flops
    )
    hidden = vmem_call(act_body, (own, *parts), shape((rows, chunk), bf16), "act")
    others = [(k, swap(hidden, "tensor", tensor_count, k)) for k in range(1, tensor_count)]
    total = vmem_call(
        functools.partial(down_body, step=0, chunk=chunk), (hidden, down_local), shape((rows, width), f32), "down0",
        flops,
    )
    for k, other in others[:-1]:
        total = vmem_call(
            functools.partial(down_body, step=k, chunk=chunk), (other, down_local, total), shape((rows, width), f32),
            f"down{k}", flops,
        )
    k, other = others[-1]
    leaving = vmem_call(
        functools.partial(last_body, step=k, chunk=chunk, ctx_count=ctx_count, capacity=capacity),
        (other, down_local, total),
        shape((expert_count * ctx_count * piece_len, width // halves), bf16),
        f"down{k}",
        flops,
    )
    back = lax.all_to_all(leaving, ("expert", "ctx"), 0, 0, tiled=True)
    return vmem_call(
        functools.partial(mix_body, ctx_count=ctx_count, piece_len=piece_len),
        (back, pick, gate),
        shape((block_len, width), bf16),
        "mix",
    )


def solution(mesh):
    body = functools.partial(
        local,
        expert_count=mesh.shape["expert"],
        ctx_count=mesh.shape["ctx"],
        tensor_count=mesh.shape["tensor"],
    )
    in_specs = (
        P("expert", "tensor"),
        P("expert", None),
        P("expert", None),
        P("expert", "ctx", "tensor"),
        P("expert", "ctx", "tensor"),
    )
    out_specs = P(("expert", "ctx"), "tensor")
    return jax.shard_map(body, mesh=mesh, in_specs=in_specs, out_specs=out_specs, check_vma=False)
```
